32 devices in a mesh: gx: 4 (over y, x), gy: 8 (over z, core).
Axes of the slice: x: 2, y: 2, z: 4, core: 2. Of those that a mesh axis runs over, the one named last changes fastest.
Arguments:
- grad_out: bfloat16 [16, 16, 64, 256], P('gx', 'gy'), may hold values from -6 to 6
- relu_mask: int32 [16, 16, 64, 256], P('gx', 'gy'), may hold values 0 or 1
- activations: bfloat16 [16, 16, 64, 256], P('gx', 'gy'), may hold values from -6 to 6
- weight: bfloat16 [27, 256, 256], P(None, 'gx'), may hold values from -0.078125 to 0.078125
Outputs:
- grad_input: bfloat16 [16, 16, 64, 256], P('gx', 'gy')
- weight_grad: float32 [27, 256, 256], P(None, 'gx', 'gy')
The draws below stay inside these ranges and needn't reach their ends.
All inputs are finite; a program needn't handle non-finite values. No bound on the sum of `relu_mask` on one device may be relied on, other than what follows from the above.
Results may differ from the reference program's by a relative error of at most 0.001.
Values may be sent and summed in bfloat16 or wider, within the bound.
A program may use at most 64 MiB of HBM per device.

```python
import math
import jax
import jax.numpy as jnp
from jax import lax

CIN = 256
COUT = 256
CX = 4
CY = 2
CZ = 64
NX = 16
NY = 16
N_GX = 4
N_GY = 8


def place_ends(values, stream_key, least, largest):
    place = [jax.random.randint(jax.random.fold_in(stream_key, axis), (), 0, length) for axis, length in enumerate(values.shape)]
    main_axis = values.shape.index(max(values.shape))
    neighbour = place[:main_axis] + [(place[main_axis] + 1) % values.shape[main_axis]] + place[main_axis + 1:]
    return values.at[tuple(place)].set(least).at[tuple(neighbour)].set(largest)


def spiked(result, key, source, target, parts, factor):
    owner, partner = [(jnp.arange(result.shape[dim]) // (result.shape[dim] // parts)).reshape([-1 if axis == dim else 1 for axis in range(result.ndim)]) for dim in (source, target)]
    chosen = jax.random.permutation(key, parts)[partner]
    strong = (owner == chosen) | (owner == (partner + parts // 2) % parts)
    return jnp.where(strong, factor * result, result)


def steps_of(stream_key, shape, cuts, least, largest):
    loudness, own = 1.0, jax.random.fold_in(stream_key, 6)
    for position, parts in cuts:
        steps = jnp.exp(jax.random.uniform(jax.random.fold_in(own, position), (parts,), jnp.float32, least / len(cuts), largest / len(cuts)))
        loudness = loudness * jnp.repeat(steps, shape[position] // parts).reshape([-1 if axis == position else 1 for axis in range(len(shape))])
    return loudness


def gaussian(own_key, extent, width, reach, cuts=(), kind=jnp.bfloat16):
    drawn = jax.random.normal(own_key, extent, jnp.float32) * width
    if len(cuts) > 0:
        drawn = steps_of(own_key, extent, cuts, -0.22, 0.18) * drawn
    return jnp.clip(drawn, min=-reach, max=reach).astype(kind)


def noise_with(key, dims, spread, most, shards, heavy, held_as=jnp.bfloat16):
    values = spread * jax.random.normal(key, dims, jnp.float32)
    if shards:
        values = values * steps_of(key, dims, shards, -0.22, 0.18)
    return jnp.clip(spiked(values, jax.random.fold_in(key, 3), *heavy), -most, most).astype(held_as)


def setup_inputs(seed: int = 0) -> dict:
    keys = jax.random.split(jax.random.key(seed), 5)
    return {
        "grad_out": noise_with(keys[0], (NX, NY, CZ, COUT), 1.0, 6.0, ((0, 4), (1, 8)), (1, 3, 8, 2.0)),
        "relu_mask": place_ends((jax.random.randint(keys[1], (NX, NY, CZ, COUT), 0, 2) < 1).astype(jnp.int32), jax.random.fold_in(keys[1], 1), 0, 1),
        "activations": noise_with(keys[2], (NX, NY, CZ, CIN), 1.0, 6.0, ((0, 4), (1, 8)), (0, 3, 4, 2.0)),
        "weight": gaussian(keys[3], (27, CIN, COUT), (27 * CIN) ** -0.5, 0.078125, ((1, 4),)),
    }


def tap_list():
    return [(a, b, c) for a in (-1, 0, 1) for b in (-1, 0, 1) for c in (-1, 0, 1)]

def reference(grad_out, relu_mask, activations, weight):
    gated = jnp.where(relu_mask != 0, grad_out, jnp.zeros_like(grad_out))
    nx, ny, nz = (gated.shape[0], gated.shape[1], gated.shape[2])
    grad_pad = jnp.pad(gated, ((1, 1), (1, 1), (1, 1), (0, 0)))
    accum = jnp.zeros((nx * ny * nz, CIN), jnp.float32)
    for tap, (a, b, c) in enumerate(tap_list()):
        window = grad_pad[1 - a:1 - a + nx, 1 - b:1 - b + ny, 1 - c:1 - c + nz, :].reshape(-1, COUT)
        accum = accum + jnp.dot(window, weight[tap].T, preferred_element_type=jnp.float32)
    grad_input = accum.reshape(nx, ny, nz, CIN).astype(jnp.bfloat16)
    input_pad = jnp.pad(activations, ((1, 1), (1, 1), (1, 1), (0, 0)))
    blocks = jnp.arange(N_GX * N_GY, dtype=jnp.int32)
    zero_index = jnp.zeros((), jnp.int32)

    def add_block(total, index):
        row = (index // N_GY).astype(jnp.int32)
        col = (index % N_GY).astype(jnp.int32)
        x_block = lax.dynamic_slice(input_pad, (row * CX, col * CY, zero_index, zero_index), (CX + 2, CY + 2, nz + 2, CIN))
        g_block = lax.dynamic_slice(gated, (row * CX, col * CY, zero_index, zero_index), (CX, CY, nz, COUT)).reshape(-1, COUT)
        terms = []
        for a, b, c in tap_list():
            shifted = x_block[1 + a:1 + a + CX, 1 + b:1 + b + CY, 1 + c:1 + c + nz, :].reshape(-1, CIN)
            terms.append(jnp.dot(shifted.T, g_block, preferred_element_type=jnp.float32))
        return (total + jnp.stack(terms, axis=0), None)
    total, unused = lax.scan(add_block, jnp.zeros((27, CIN, COUT), jnp.float32), blocks)
    weight_grad = total * (1.0 / math.sqrt(nx * ny * nz))
    return (grad_input, weight_grad)
```

```python
import functools
import math

import jax
import jax.numpy as jnp
from jax import lax
from jax.experimental import pallas as pl
from jax.experimental.pallas import tpu as pltpu
from jax.sharding import PartitionSpec as P

MESH = pl.DeviceIdType.MESH
ORDER = (1, 4, 7, 0, 3, 6, 2, 5, 8)
PER = 2


def kernel(nx, ny, scale, gated_ref, act_ref, w_ref, out_ref, wg_ref,
           gbuf, abuf, a3, wbuf, acc, dwt, pair, red, rs, gsend, grecv,
           loc_sem, gat_s, gat_r, act_s, act_r, halo_s, halo_r,
           pair_s, pair_r, rs_s, rs_r, gi_s, gi_r):
    g = lax.axis_index("gx")
    h = lax.axis_index("gy")
    sx, sy, sz, co = gated_ref.shape
    ish = w_ref.shape[1]
    rows = 3 * ish
    cells = sx * sy * sz
    nz = ny // 2
    z = h // 2
    core = h - 2 * z
    partner = 2 * z + 1 - core
    chunks = [ORDER[i:i + PER] for i in range(0, 9, PER)]

    def xpeer(s):
        return lax.rem(g + s, nx)

    def xfrom(s):
        return lax.rem(g + nx - s, nx)

    def zpeer(s):
        return 2 * lax.rem(z + s, nz) + core

    barrier = pltpu.get_barrier_semaphore()
    for s in range(1, nx):
        pl.semaphore_signal(barrier, inc=1, device_id=(xpeer(s), h), device_id_type=MESH)
    for s in range(1, nz):
        pl.semaphore_signal(barrier, inc=1, device_id=(g, zpeer(s)), device_id_type=MESH)
    pl.semaphore_signal(barrier, inc=1, device_id=(g, partner), device_id_type=MESH)
    outer = h + 2 * core - 1
    has_outer = jnp.logical_and(outer >= 0, outer < ny)

    @pl.when(has_outer)
    def _():
        pl.semaphore_signal(barrier, inc=1, device_id=(g, outer), device_id_type=MESH)

    mine = gbuf.at[pl.ds(1 + sx * g, sx), pl.ds(1, sy)]
    own_g = pltpu.make_async_copy(gated_ref, mine, loc_sem.at[0])
    own_a = pltpu.make_async_copy(act_ref.at[g], abuf.at[g], loc_sem.at[1])
    own_w = pltpu.make_async_copy(w_ref, wbuf, loc_sem.at[2])
    own_g.start()
    own_a.start()
    own_w.start()
    gbuf[0] = jnp.zeros(gbuf.shape[1:], gbuf.dtype)
    gbuf[sx * nx + 1] = jnp.zeros(gbuf.shape[1:], gbuf.dtype)

    @pl.when(h == 0)
    def _():
        gbuf[pl.ds(1, sx * nx), 0] = jnp.zeros((sx * nx, sz, co), gbuf.dtype)

    @pl.when(h == ny - 1)
    def _():
        gbuf[pl.ds(1, sx * nx), sy + 1] = jnp.zeros((sx * nx, sz, co), gbuf.dtype)

    pl.semaphore_wait(barrier, nx - 1 + nz - 1 + 1 + has_outer.astype(jnp.int32))

    gat = {}
    acts = {}
    for s in range(1, nx):
        gat[s] = pltpu.make_async_remote_copy(
            src_ref=gated_ref, dst_ref=mine, send_sem=gat_s.at[s], recv_sem=gat_r.at[s],
            device_id=(xpeer(s), h), device_id_type=MESH)
        gat[s].start()
    for s in range(1, nx):
        acts[s] = pltpu.make_async_remote_copy(
            src_ref=act_ref.at[xpeer(s)], dst_ref=abuf.at[g], send_sem=act_s.at[s],
            recv_sem=act_r.at[s], device_id=(xpeer(s), h), device_id_type=MESH)
        acts[s].start()

    def halo(s, up):
        block = pl.ds(1 + sx * xfrom(s), sx)
        src = gbuf.at[block, sy] if up else gbuf.at[block, 1]
        dst = gbuf.at[block, 0] if up else gbuf.at[block, sy + 1]
        k = 0 if up else 1
        return pltpu.make_async_remote_copy(
            src_ref=src, dst_ref=dst, send_sem=halo_s.at[k, s], recv_sem=halo_r.at[k, s],
            device_id=(g, h + 1 if up else h - 1), device_id_type=MESH)

    own_g.wait()
    for s in range(nx):
        if s > 0:
            gat[s].wait_recv()

        @pl.when(h < ny - 1)
        def _():
            halo(s, True).start()

        @pl.when(h > 0)
        def _():
            halo(s, False).start()

    lane = lax.broadcasted_iota(jnp.int32, (ish, cells), 1)
    zpos = lax.rem(lane, sz)
    own_a.wait()
    for s in range(nx):
        if s > 0:
            acts[s].wait_recv()
        p = xfrom(s)
        v = abuf[p].astype(jnp.float32)
        a3[p, pl.ds(0, ish)] = jnp.where(
            zpos >= 1, pltpu.roll(v, 1, 1), 0.0).astype(jnp.bfloat16)
        a3[p, pl.ds(ish, ish)] = v.astype(jnp.bfloat16)
        a3[p, pl.ds(2 * ish, ish)] = jnp.where(
            zpos <= sz - 2, pltpu.roll(v, cells - 1, 1), 0.0).astype(jnp.bfloat16)
    own_w.wait()

    def window(ab, p):
        a = ab // 3 - 1
        b = ab - 3 * (ab // 3) - 1
        return gbuf[pl.ds(1 - a + sx * p, sx), pl.ds(1 - b, sy)].reshape(cells, co)

    def pair_copy(k, width):
        return pltpu.make_async_remote_copy(
            src_ref=dwt.at[k, :, 1 - core, :, pl.ds(0, width)],
            dst_ref=pair.at[k, :, :, pl.ds(0, width)],
            send_sem=pair_s.at[k], recv_sem=pair_r.at[k],
            device_id=(g, partner), device_id_type=MESH)

    def rs_copy(k, s, width):
        return pltpu.make_async_remote_copy(
            src_ref=red.at[k, lax.rem(z + s, nz), :, pl.ds(0, width)],
            dst_ref=rs.at[k, s, :, pl.ds(0, width)],
            send_sem=rs_s.at[k, s], recv_sem=rs_r.at[k, s],
            device_id=(g, zpeer(s)), device_id_type=MESH)

    widths = [-(-len(c) * rows // 128) * 128 for c in chunks]

    def finish_pair(k):
        w = widths[k]
        pair_copy(k, w).wait_recv()
        red[k, :, :, pl.ds(0, w)] = dwt[k, :, core, :, pl.ds(0, w)] + pair[k, :, :, pl.ds(0, w)]
        for s in range(1, nz):
            rs_copy(k, s, w).start()

    seen_halo = False
    for k, chunk in enumerate(chunks):
        for j, ab in enumerate(chunk):
            if ab % 3 != 1 and not seen_halo:
                seen_halo = True

                @pl.when(h > 0)
                def _():
                    for s in range(nx):
                        halo(s, True).wait_recv()

                @pl.when(h < ny - 1)
                def _():
                    for s in range(nx):
                        halo(s, False).wait_recv()

            def step(p, total, ab=ab):
                return total + jnp.dot(a3[p], window(ab, p), preferred_element_type=jnp.float32)
            total = lax.fori_loop(
                0, nx, step, jnp.zeros((rows, co), jnp.float32), unroll=nx <= 4)
            acc[k, pl.ds(j * rows, rows)] = total
        used = len(chunk) * rows
        if used < widths[k]:
            acc[k, pl.ds(used, widths[k] - used)] = jnp.zeros((widths[k] - used, co), jnp.float32)
        w = widths[k]
        dwt[k, :, :, :, pl.ds(0, w)] = acc[k, pl.ds(0, w)].T.reshape(nz, 2, co // ny, w)
        pair_copy(k, w).start()
        if k > 0:
            finish_pair(k - 1)
    finish_pair(len(chunks) - 1)

    def gi_copy(s):
        return pltpu.make_async_remote_copy(
            src_ref=gsend.at[s], dst_ref=grecv.at[g], send_sem=gi_s.at[s], recv_sem=gi_r.at[s],
            device_id=(xpeer(s), h), device_id_type=MESH)

    def shifted(p):
        def step(ab, total):
            return total + lax.dot_general(
                wbuf[pl.ds(3 * ab, 3)].reshape(rows, co), window(ab, p),
                (((1,), (1,)), ((), ())), preferred_element_type=jnp.float32)
        prod = lax.fori_loop(0, 9, step, jnp.zeros((rows, cells), jnp.float32))
        low = jnp.where(zpos <= sz - 2, pltpu.roll(prod[:ish], cells - 1, 1), 0.0)
        high = jnp.where(zpos >= 1, pltpu.roll(prod[2 * ish:], 1, 1), 0.0)
        return (prod[ish:2 * ish] + low + high).astype(jnp.bfloat16)

    for s in range(1, nx):
        gsend[s] = shifted(xpeer(s))
        gi_copy(s).start()
    grecv[g] = shifted(g)

    for s in range(1, nx):
        gi_copy(s).wait_recv()
    full = grecv[...].reshape(nx * ish, cells).astype(jnp.float32)
    out_ref[...] = full.T.astype(jnp.bfloat16).reshape(sx, sy, sz, nx * ish)
    for k, chunk in enumerate(chunks):
        w = widths[k]
        total = red[k, z, :, pl.ds(0, w)]
        for s in range(1, nz):
            rs_copy(k, s, w).wait_recv()
            total = total + rs[k, s, :, pl.ds(0, w)]
        block = (total * scale).T
        for j, ab in enumerate(chunk):
            wg_ref[pl.ds(3 * ab, 3)] = block[j * rows:(j + 1) * rows].reshape(3, ish, co // ny)

    for s in range(1, nx):
        gat[s].wait_send()
        acts[s].wait_send()
        gi_copy(s).wait_send()

    @pl.when(h < ny - 1)
    def _():
        for s in range(nx):
            halo(s, True).wait_send()

    @pl.when(h > 0)
    def _():
        for s in range(nx):
            halo(s, False).wait_send()

    for k in range(len(chunks)):
        pair_copy(k, widths[k]).wait_send()
        for s in range(1, nz):
            rs_copy(k, s, widths[k]).wait_send()


def body(nx, ny, grad_out, relu_mask, activations, weight):
    sx, sy, sz, co = grad_out.shape
    ish = weight.shape[1]
    rows = 3 * ish
    cells = sx * sy * sz
    nz = ny // 2
    nch = -(-9 // PER)
    wide = -(-PER * rows // 128) * 128
    gated = jnp.where(relu_mask != 0, grad_out, jnp.zeros_like(grad_out))
    act_t = activations.reshape(cells, nx * ish).T.reshape(nx, ish, cells)
    scale = 1.0 / math.sqrt(cells * nx * ny)
    dma = pltpu.SemaphoreType.DMA
    bf, f32 = jnp.bfloat16, jnp.float32
    any_spec = pl.BlockSpec(memory_space=pl.ANY)
    vmem_spec = pl.BlockSpec(memory_space=pltpu.VMEM)
    out, wg = pl.pallas_call(
        functools.partial(kernel, nx, ny, scale),
        out_shape=(jax.ShapeDtypeStruct((sx, sy, sz, nx * ish), bf),
                   jax.ShapeDtypeStruct((27, ish, co // ny), f32)),
        in_specs=[any_spec] * 3,
        out_specs=(vmem_spec, vmem_spec),
        scratch_shapes=[
            pltpu.VMEM((sx * nx + 2, sy + 2, sz, co), bf),
            pltpu.VMEM((nx, ish, cells), bf),
            pltpu.VMEM((nx, rows, cells), bf),
            pltpu.VMEM((27, ish, co), bf),
            pltpu.VMEM((nch, wide, co), f32),
            pltpu.VMEM((nch, nz, 2, co // ny, wide), f32),
            pltpu.VMEM((nch, nz, co // ny, wide), f32),
            pltpu.VMEM((nch, nz, co // ny, wide), f32),
            pltpu.VMEM((nch, nz, co // ny, wide), f32),
            pltpu.VMEM((nx, ish, cells), bf),
            pltpu.VMEM((nx, ish, cells), bf),
            dma((3,)), dma((nx,)), dma((nx,)), dma((nx,)), dma((nx,)),
            dma((2, nx)), dma((2, nx)), dma((nch,)), dma((nch,)),
            dma((nch, nz)), dma((nch, nz)), dma((nx,)), dma((nx,)),
        ],
        compiler_params=pltpu.CompilerParams(
            collective_id=0, has_side_effects=True, vmem_limit_bytes=60 * 1024 * 1024),
        name="conv_backward",
    )(gated, act_t, weight)
    return out, wg


def solution(mesh):
    nx, ny = mesh.shape["gx"], mesh.shape["gy"]
    in_specs = (
        P("gx", "gy", None, None),
        P("gx", "gy", None, None),
        P("gx", "gy", None, None),
        P(None, "gx", None),
    )
    out_specs = (P("gx", "gy", None, None), P(None, "gx", "gy"))
    return jax.shard_map(
        functools.partial(body, nx, ny), mesh=mesh, in_specs=in_specs, out_specs=out_specs,
        check_vma=False)
```

```python
import functools
import math

import jax
import jax.numpy as jnp
from jax import lax
from jax.experimental import pallas as pl
from jax.experimental.pallas import tpu as pltpu
from jax.sharding import PartitionSpec as P

MESH = pl.DeviceIdType.MESH
ORDER = (1, 4, 7, 0, 3, 6, 2, 5, 8)
PER = 2
CHUNKS = [ORDER[i:i + PER] for i in range(0, 9, PER)]
NCH = len(CHUNKS)
LAG = 2


def kernel(nx, ny, nbits, scale, *refs):
    (grad_ref, mask_ref, act_ref, w_ref, out_ref, wg_ref,
     gin, min_, ain, gbuf, asend, abuf, a3, wbuf, wp, acc, dwt, pair, gsend, grecv) = refs[:20]
    curs = refs[20:20 + nbits - 1]
    recvs = refs[20 + nbits - 1:20 + 2 * (nbits - 1)]
    (loc_sem, gat_s, gat_r, act_s, act_r, halo_s, halo_r,
     pair_s, pair_r, rs_s, rs_r, gi_s, gi_r) = refs[20 + 2 * (nbits - 1):]
    g = lax.axis_index("gx")
    h = lax.axis_index("gy")
    sx, sy, sz, co = gin.shape
    ish = w_ref.shape[1]
    osh = co // ny
    hc = co // 2
    rows = 3 * ish
    cells = sx * sy * sz
    f32, bf = jnp.float32, jnp.bfloat16
    core = lax.rem(h, 2)
    bits = [lax.rem(h // 2 ** j, 2) for j in range(nbits)]
    partners = [h + 2 ** j * (1 - 2 * bits[j]) for j in range(nbits)]

    def xpeer(s):
        return lax.rem(g + s, nx)

    def xfrom(s):
        return lax.rem(g + nx - s, nx)

    in_g = pltpu.make_async_copy(grad_ref, gin, loc_sem.at[0])
    in_m = pltpu.make_async_copy(mask_ref, min_, loc_sem.at[1])
    in_a = pltpu.make_async_copy(act_ref, ain, loc_sem.at[2])
    in_w = pltpu.make_async_copy(w_ref, wbuf, loc_sem.at[3])
    in_m.start()
    in_g.start()
    in_a.start()
    in_w.start()

    barrier = pltpu.get_barrier_semaphore()
    for s in range(1, nx):
        pl.semaphore_signal(barrier, inc=1, device_id=(xpeer(s), h), device_id_type=MESH)
    for j in range(nbits):
        pl.semaphore_signal(barrier, inc=1, device_id=(g, partners[j]), device_id_type=MESH)
    outer = h + 2 * core - 1
    has_outer = jnp.logical_and(outer >= 0, outer < ny)

    @pl.when(has_outer)
    def _():
        pl.semaphore_signal(barrier, inc=1, device_id=(g, outer), device_id_type=MESH)

    o_in = lax.broadcasted_iota(jnp.int32, (co, co), 0)
    o_out = lax.broadcasted_iota(jnp.int32, (co, co), 1)
    owner = lax.div(o_in, osh)
    place = lax.rem(owner, 2) * hc + lax.div(owner, 2) * osh + lax.rem(o_in, osh)
    perm = jnp.where(place == o_out, 1.0, 0.0).astype(bf)

    in_m.wait()
    in_g.wait()
    gated = jnp.where(min_[...].reshape(cells, co) != 0,
                      gin[...].reshape(cells, co).astype(f32), 0.0).astype(bf)
    ordered = jnp.dot(gated, perm, preferred_element_type=f32).astype(bf)
    mine = (pl.ds(1 + sx * g, sx), pl.ds(1, sy))
    for q in range(2):
        gbuf[(q,) + mine] = ordered[:, q * hc:(q + 1) * hc].reshape(sx, sy, sz, hc)
    in_a.wait()
    asend[...] = ain[...].reshape(cells, nx * ish).astype(f32).T.astype(bf).reshape(
        nx, ish, cells)

    pl.semaphore_wait(barrier, nx - 1 + nbits + has_outer.astype(jnp.int32))

    gat = {}
    acts = {}
    for s in range(1, nx):
        acts[s] = pltpu.make_async_remote_copy(
            src_ref=asend.at[xpeer(s)], dst_ref=abuf.at[g], send_sem=act_s.at[s],
            recv_sem=act_r.at[s], device_id=(xpeer(s), h), device_id_type=MESH)
        acts[s].start()
    for q in range(2):
        for s in range(1, nx):
            gat[q, s] = pltpu.make_async_remote_copy(
                src_ref=gbuf.at[(q,) + mine], dst_ref=gbuf.at[(q,) + mine],
                send_sem=gat_s.at[q, s], recv_sem=gat_r.at[q, s],
                device_id=(xpeer(s), h), device_id_type=MESH)
            gat[q, s].start()

    def halo(q, s, up):
        block = pl.ds(1 + sx * xfrom(s), sx)
        src = gbuf.at[q, block, sy] if up else gbuf.at[q, block, 1]
        dst = gbuf.at[q, block, 0] if up else gbuf.at[q, block, sy + 1]
        k = 0 if up else 1
        return pltpu.make_async_remote_copy(
            src_ref=src, dst_ref=dst, send_sem=halo_s.at[q, k, s], recv_sem=halo_r.at[q, k, s],
            device_id=(g, h + 1 if up else h - 1), device_id_type=MESH)

    def forward(q, s):
        @pl.when(h < ny - 1)
        def _():
            halo(q, s, True).start()

        @pl.when(h > 0)
        def _():
            halo(q, s, False).start()

    forward(0, 0)
    forward(1, 0)
    for q in range(2):
        gbuf[q, 0] = jnp.zeros((sy + 2, sz, hc), bf)
        gbuf[q, sx * nx + 1] = jnp.zeros((sy + 2, sz, hc), bf)

        @pl.when(h == 0)
        def _():
            gbuf[q, pl.ds(1, sx * nx), 0] = jnp.zeros((sx * nx, sz, hc), bf)

        @pl.when(h == ny - 1)
        def _():
            gbuf[q, pl.ds(1, sx * nx), sy + 1] = jnp.zeros((sx * nx, sz, hc), bf)

    in_w.wait()
    wp[...] = jnp.dot(wbuf[...].reshape(27 * ish, co), perm,
                      preferred_element_type=f32).astype(bf).reshape(27, ish, co)

    zpos = lax.rem(lax.broadcasted_iota(jnp.int32, (ish, cells), 1), sz)

    def spread(p, v):
        v = v.astype(f32)
        a3[p, pl.ds(0, ish)] = jnp.where(zpos >= 1, pltpu.roll(v, 1, 1), 0.0).astype(bf)
        a3[p, pl.ds(ish, ish)] = v.astype(bf)
        a3[p, pl.ds(2 * ish, ish)] = jnp.where(
            zpos <= sz - 2, pltpu.roll(v, cells - 1, 1), 0.0).astype(bf)

    spread(g, asend[g])
    for s in range(1, nx):
        acts[s].wait_recv()
        spread(xfrom(s), abuf[xfrom(s)])

    def window(q, ab, p):
        a = ab // 3 - 1
        b = ab - 3 * (ab // 3) - 1
        return gbuf[q, pl.ds(1 - a + sx * p, sx), pl.ds(1 - b, sy)].reshape(cells, hc)

    widths = [-(-len(c) * rows // 128) * 128 for c in CHUNKS]
    steps = [(q, k) for q in range(2) for k in range(NCH)]

    def pair_copy(q, k):
        w = widths[k]
        return pltpu.make_async_remote_copy(
            src_ref=dwt.at[q, k, :, :, pl.ds(0, w)], dst_ref=pair.at[k, :, :, pl.ds(0, w)],
            send_sem=pair_s.at[k], recv_sem=pair_r.at[k],
            device_id=(g, partners[0]), device_id_type=MESH)

    def stage_copy(k, j):
        w = widths[k]
        return pltpu.make_async_remote_copy(
            src_ref=curs[j - 1].at[k, :, 1 - bits[j], :, pl.ds(0, w)],
            dst_ref=recvs[j - 1].at[k, :, :, pl.ds(0, w)],
            send_sem=rs_s.at[k, j], recv_sem=rs_r.at[k, j],
            device_id=(g, partners[j]), device_id_type=MESH)

    def arrived(q, k, j):
        w = widths[k]
        if j == 0:
            pair_copy(q, k).wait_recv()
            return dwt[q, k, :, :, pl.ds(0, w)] + pair[k, :, :, pl.ds(0, w)]
        stage_copy(k, j).wait_recv()
        return (curs[j - 1][k, :, bits[j], :, pl.ds(0, w)]
                + recvs[j - 1][k, :, :, pl.ds(0, w)])

    def advance(q, k, j):
        @pl.when(core == q)
        def _():
            total = arrived(q, k, j)
            n = total.shape[0]
            curs[j][k, :, :, :, pl.ds(0, widths[k])] = total.reshape(
                n // 2, 2, osh, widths[k])
            stage_copy(k, j + 1).start()

    todo = [(i + 1 + LAG * j, i, j) for i in range(len(steps)) for j in range(nbits - 1)]
    todo.sort()

    def progress(now):
        while todo and todo[0][0] <= now:
            _, i, j = todo.pop(0)
            advance(steps[i][0], steps[i][1], j)

    def halo_wait(q):
        @pl.when(h > 0)
        def _():
            for s in range(nx):
                halo(q, s, True).wait_recv()

        @pl.when(h < ny - 1)
        def _():
            for s in range(nx):
                halo(q, s, False).wait_recv()

    for i, (q, k) in enumerate(steps):
        if k == 0:
            for s in range(1, nx):
                gat[q, s].wait_recv()
                forward(q, s)
        for j, ab in enumerate(CHUNKS[k]):
            if ORDER.index(ab) == 3:
                halo_wait(q)

            def step(p, total, ab=ab, q=q):
                return total + jnp.dot(a3[p], window(q, ab, p), preferred_element_type=f32)
            acc[pl.ds(j * rows, rows)] = lax.fori_loop(
                0, nx, step, jnp.zeros((rows, hc), f32), unroll=nx <= 4)
        used, w = len(CHUNKS[k]) * rows, widths[k]
        if used < w:
            acc[pl.ds(used, w - used)] = jnp.zeros((w - used, hc), f32)
        dwt[q, k, :, :, pl.ds(0, w)] = acc[pl.ds(0, w)].T.reshape(ny // 2, osh, w)

        @pl.when(core != q)
        def _():
            pair_copy(q, k).start()
        progress(i)

    def gi_copy(s):
        return pltpu.make_async_remote_copy(
            src_ref=gsend.at[s], dst_ref=grecv.at[g], send_sem=gi_s.at[s], recv_sem=gi_r.at[s],
            device_id=(xpeer(s), h), device_id_type=MESH)

    def shifted(p):
        def step(ab, total):
            both = jnp.concatenate([window(0, ab, p), window(1, ab, p)], axis=1)
            return total + lax.dot_general(
                wp[pl.ds(3 * ab, 3)].reshape(rows, co), both,
                (((1,), (1,)), ((), ())), preferred_element_type=f32)
        prod = lax.fori_loop(0, 9, step, jnp.zeros((rows, cells), f32))
        low = jnp.where(zpos <= sz - 2, pltpu.roll(prod[:ish], cells - 1, 1), 0.0)
        high = jnp.where(zpos >= 1, pltpu.roll(prod[2 * ish:], 1, 1), 0.0)
        return (prod[ish:2 * ish] + low + high).astype(bf)

    for s in range(1, nx):
        gsend[s] = shifted(xpeer(s))
        gi_copy(s).start()
        progress(len(steps) - 1 + s)
    grecv[g] = shifted(g)
    progress(10 ** 6)

    for s in range(1, nx):
        gi_copy(s).wait_recv()
    full = grecv[...].reshape(nx * ish, cells).astype(f32)
    out_ref[...] = full.T.astype(bf).reshape(sx, sy, sz, nx * ish)
    for k, chunk in enumerate(CHUNKS):
        block = arrived(None, k, nbits - 1)[0] * scale
        for j, ab in enumerate(chunk):
            for c in range(3):
                lane = j * rows + c * ish
                wg_ref[3 * ab + c] = block[:, lane:lane + ish]

    for s in range(1, nx):
        gat[0, s].wait_send()
        gat[1, s].wait_send()
        acts[s].wait_send()
        gi_copy(s).wait_send()

    for q in range(2):
        @pl.when(h < ny - 1)
        def _():
            for s in range(nx):
                halo(q, s, True).wait_send()

        @pl.when(h > 0)
        def _():
            for s in range(nx):
                halo(q, s, False).wait_send()

    for k in range(NCH):
        pair_copy(1 - core, k).wait_send()
        for j in range(1, nbits):
            stage_copy(k, j).wait_send()


def body(nx, ny, grad_out, relu_mask, activations, weight):
    sx, sy, sz, co = grad_out.shape
    ish = weight.shape[1]
    rows = 3 * ish
    cells = sx * sy * sz
    osh = co // ny
    nbits = ny.bit_length() - 1
    assert ny == 2 ** nbits and nbits >= 2
    wide = -(-PER * rows // 128) * 128
    scale = 1.0 / math.sqrt(cells * nx * ny)
    dma = pltpu.SemaphoreType.DMA
    bf, f32 = jnp.bfloat16, jnp.float32
    any_spec = pl.BlockSpec(memory_space=pl.ANY)
    vmem_spec = pl.BlockSpec(memory_space=pltpu.VMEM)
    sizes = [ny // 2 ** (j + 2) for j in range(nbits - 1)]
    out, wg = pl.pallas_call(
        functools.partial(kernel, nx, ny, nbits, scale),
        out_shape=(jax.ShapeDtypeStruct((sx, sy, sz, nx * ish), bf),
                   jax.ShapeDtypeStruct((27, osh, ish), f32)),
        in_specs=[any_spec] * 4,
        out_specs=(vmem_spec, vmem_spec),
        scratch_shapes=[
            pltpu.VMEM((sx, sy, sz, co), bf),
            pltpu.VMEM((sx, sy, sz, co), jnp.int32),
            pltpu.VMEM((sx, sy, sz, nx * ish), bf),
            pltpu.VMEM((2, sx * nx + 2, sy + 2, sz, co // 2), bf),
            pltpu.VMEM((nx, ish, cells), bf),
            pltpu.VMEM((nx, ish, cells), bf),
            pltpu.VMEM((nx, rows, cells), bf),
            pltpu.VMEM((27, ish, co), bf),
            pltpu.VMEM((27, ish, co), bf),
            pltpu.VMEM((wide, co // 2), f32),
            pltpu.VMEM((2, NCH, ny // 2, osh, wide), f32),
            pltpu.VMEM((NCH, ny // 2, osh, wide), f32),
            pltpu.VMEM((nx, ish, cells), bf),
            pltpu.VMEM((nx, ish, cells), bf),
            *[pltpu.VMEM((NCH, n, 2, osh, wide), f32) for n in sizes],
            *[pltpu.VMEM((NCH, n, osh, wide), f32) for n in sizes],
            dma((4,)), dma((2, nx)), dma((2, nx)), dma((nx,)), dma((nx,)),
            dma((2, 2, nx)), dma((2, 2, nx)), dma((NCH,)), dma((NCH,)),
            dma((NCH, nbits)), dma((NCH, nbits)), dma((nx,)), dma((nx,)),
        ],
        compiler_params=pltpu.CompilerParams(
            collective_id=0, has_side_effects=True, vmem_limit_bytes=60 * 1024 * 1024),
        name="conv_backward",
    )(grad_out, relu_mask, activations, weight)
    return out, jnp.transpose(wg, (0, 2, 1))


def solution(mesh):
    nx, ny = mesh.shape["gx"], mesh.shape["gy"]
    in_specs = (
        P("gx", "gy", None, None),
        P("gx", "gy", None, None),
        P("gx", "gy", None, None),
        P(None, "gx", None),
    )
    out_specs = (P("gx", "gy", None, None), P(None, "gx", "gy"))
    return jax.shard_map(
        functools.partial(body, nx, ny), mesh=mesh, in_specs=in_specs, out_specs=out_specs,
        check_vma=False)
```

```python
import functools
import math

import jax
import jax.numpy as jnp
from jax import lax
from jax.experimental import pallas as pl
from jax.experimental.pallas import tpu as pltpu
from jax.sharding import PartitionSpec as P

MESH = pl.DeviceIdType.MESH
ORDER = (1, 4, 7, 0, 3, 6, 2, 5, 8)
PER = 2


def kernel(nx, ny, scale, grad_ref, mask_ref, act_ref, w_ref, out_ref, wg_ref,
           gin, min_, ain, asend, gbuf, abuf, a3, wbuf, acc, dwt, pair, red, rs, gsend, grecv,
           loc_sem, gat_s, gat_r, act_s, act_r, halo_s, halo_r,
           pair_s, pair_r, rs_s, rs_r, gi_s, gi_r):
    g = lax.axis_index("gx")
    h = lax.axis_index("gy")
    sx, sy, sz, co = gin.shape
    ish = w_ref.shape[1]
    rows = 3 * ish
    cells = sx * sy * sz
    nz = ny // 2
    z = h // 2
    core = h - 2 * z
    partner = 2 * z + 1 - core
    chunks = [ORDER[i:i + PER] for i in range(0, 9, PER)]

    def xpeer(s):
        return lax.rem(g + s, nx)

    def xfrom(s):
        return lax.rem(g + nx - s, nx)

    def zpeer(s):
        return 2 * lax.rem(z + s, nz) + core

    in_m = pltpu.make_async_copy(mask_ref, min_, loc_sem.at[0])
    in_g = pltpu.make_async_copy(grad_ref, gin, loc_sem.at[1])
    in_a = pltpu.make_async_copy(act_ref, ain, loc_sem.at[2])
    own_w = pltpu.make_async_copy(w_ref, wbuf, loc_sem.at[3])
    in_m.start()
    in_g.start()
    in_a.start()
    own_w.start()

    barrier = pltpu.get_barrier_semaphore()
    for s in range(1, nx):
        pl.semaphore_signal(barrier, inc=1, device_id=(xpeer(s), h), device_id_type=MESH)
    for s in range(1, nz):
        pl.semaphore_signal(barrier, inc=1, device_id=(g, zpeer(s)), device_id_type=MESH)
    pl.semaphore_signal(barrier, inc=1, device_id=(g, partner), device_id_type=MESH)
    outer = h + 2 * core - 1
    has_outer = jnp.logical_and(outer >= 0, outer < ny)

    @pl.when(has_outer)
    def _():
        pl.semaphore_signal(barrier, inc=1, device_id=(g, outer), device_id_type=MESH)

    mine = gbuf.at[pl.ds(1 + sx * g, sx), pl.ds(1, sy)]
    in_m.wait()
    in_g.wait()
    gbuf[pl.ds(1 + sx * g, sx), pl.ds(1, sy)] = jnp.where(
        min_[...].reshape(cells, co) != 0, gin[...].reshape(cells, co).astype(jnp.float32),
        0.0).astype(jnp.bfloat16).reshape(sx, sy, sz, co)
    in_a.wait()
    asend[...] = ain[...].reshape(cells, nx * ish).astype(jnp.float32).T.astype(
        jnp.bfloat16).reshape(nx, ish, cells)
    gbuf[0] = jnp.zeros(gbuf.shape[1:], gbuf.dtype)
    gbuf[sx * nx + 1] = jnp.zeros(gbuf.shape[1:], gbuf.dtype)

    @pl.when(h == 0)
    def _():
        gbuf[pl.ds(1, sx * nx), 0] = jnp.zeros((sx * nx, sz, co), gbuf.dtype)

    @pl.when(h == ny - 1)
    def _():
        gbuf[pl.ds(1, sx * nx), sy + 1] = jnp.zeros((sx * nx, sz, co), gbuf.dtype)

    pl.semaphore_wait(barrier, nx - 1 + nz - 1 + 1 + has_outer.astype(jnp.int32))

    gat = {}
    acts = {}
    for s in range(1, nx):
        gat[s] = pltpu.make_async_remote_copy(
            src_ref=mine, dst_ref=mine, send_sem=gat_s.at[s], recv_sem=gat_r.at[s],
            device_id=(xpeer(s), h), device_id_type=MESH)
        gat[s].start()
    for s in range(1, nx):
        acts[s] = pltpu.make_async_remote_copy(
            src_ref=asend.at[xpeer(s)], dst_ref=abuf.at[g], send_sem=act_s.at[s],
            recv_sem=act_r.at[s], device_id=(xpeer(s), h), device_id_type=MESH)
        acts[s].start()

    def halo(s, up):
        block = pl.ds(1 + sx * xfrom(s), sx)
        src = gbuf.at[block, sy] if up else gbuf.at[block, 1]
        dst = gbuf.at[block, 0] if up else gbuf.at[block, sy + 1]
        k = 0 if up else 1
        return pltpu.make_async_remote_copy(
            src_ref=src, dst_ref=dst, send_sem=halo_s.at[k, s], recv_sem=halo_r.at[k, s],
            device_id=(g, h + 1 if up else h - 1), device_id_type=MESH)

    for s in range(nx):
        if s > 0:
            gat[s].wait_recv()

        @pl.when(h < ny - 1)
        def _():
            halo(s, True).start()

        @pl.when(h > 0)
        def _():
            halo(s, False).start()

    lane = lax.broadcasted_iota(jnp.int32, (ish, cells), 1)
    zpos = lax.rem(lane, sz)
    for s in range(nx):
        if s > 0:
            acts[s].wait_recv()
        p = xfrom(s)
        v = (abuf[p] if s > 0 else asend[p]).astype(jnp.float32)
        a3[p, pl.ds(0, ish)] = jnp.where(
            zpos >= 1, pltpu.roll(v, 1, 1), 0.0).astype(jnp.bfloat16)
        a3[p, pl.ds(ish, ish)] = v.astype(jnp.bfloat16)
        a3[p, pl.ds(2 * ish, ish)] = jnp.where(
            zpos <= sz - 2, pltpu.roll(v, cells - 1, 1), 0.0).astype(jnp.bfloat16)
    own_w.wait()

    def window(ab, p):
        a = ab // 3 - 1
        b = ab - 3 * (ab // 3) - 1
        return gbuf[pl.ds(1 - a + sx * p, sx), pl.ds(1 - b, sy)].reshape(cells, co)

    def pair_copy(k, width):
        return pltpu.make_async_remote_copy(
            src_ref=dwt.at[k, :, 1 - core, :, pl.ds(0, width)],
            dst_ref=pair.at[k, :, :, pl.ds(0, width)],
            send_sem=pair_s.at[k], recv_sem=pair_r.at[k],
            device_id=(g, partner), device_id_type=MESH)

    def rs_copy(k, s, width):
        return pltpu.make_async_remote_copy(
            src_ref=red.at[k, lax.rem(z + s, nz), :, pl.ds(0, width)],
            dst_ref=rs.at[k, s, :, pl.ds(0, width)],
            send_sem=rs_s.at[k, s], recv_sem=rs_r.at[k, s],
            device_id=(g, zpeer(s)), device_id_type=MESH)

    widths = [-(-len(c) * rows // 128) * 128 for c in chunks]

    def finish_pair(k):
        w = widths[k]
        pair_copy(k, w).wait_recv()
        red[k, :, :, pl.ds(0, w)] = dwt[k, :, core, :, pl.ds(0, w)] + pair[k, :, :, pl.ds(0, w)]
        for s in range(1, nz):
            rs_copy(k, s, w).start()

    seen_halo = False
    for k, chunk in enumerate(chunks):
        for j, ab in enumerate(chunk):
            if ab % 3 != 1 and not seen_halo:
                seen_halo = True

                @pl.when(h > 0)
                def _():
                    for s in range(nx):
                        halo(s, True).wait_recv()

                @pl.when(h < ny - 1)
                def _():
                    for s in range(nx):
                        halo(s, False).wait_recv()

            def step(p, total, ab=ab):
                return total + jnp.dot(a3[p], window(ab, p), preferred_element_type=jnp.float32)
            total = lax.fori_loop(
                0, nx, step, jnp.zeros((rows, co), jnp.float32), unroll=nx <= 4)
            acc[k, pl.ds(j * rows, rows)] = total
        used = len(chunk) * rows
        if used < widths[k]:
            acc[k, pl.ds(used, widths[k] - used)] = jnp.zeros((widths[k] - used, co), jnp.float32)
        w = widths[k]
        dwt[k, :, :, :, pl.ds(0, w)] = acc[k, pl.ds(0, w)].T.reshape(nz, 2, co // ny, w)
        pair_copy(k, w).start()
        if k > 0:
            finish_pair(k - 1)
    finish_pair(len(chunks) - 1)

    def gi_copy(s):
        return pltpu.make_async_remote_copy(
            src_ref=gsend.at[s], dst_ref=grecv.at[g], send_sem=gi_s.at[s], recv_sem=gi_r.at[s],
            device_id=(xpeer(s), h), device_id_type=MESH)

    def shifted(p):
        def step(ab, total):
            return total + lax.dot_general(
                wbuf[pl.ds(3 * ab, 3)].reshape(rows, co), window(ab, p),
                (((1,), (1,)), ((), ())), preferred_element_type=jnp.float32)
        prod = lax.fori_loop(0, 9, step, jnp.zeros((rows, cells), jnp.float32))
        low = jnp.where(zpos <= sz - 2, pltpu.roll(prod[:ish], cells - 1, 1), 0.0)
        high = jnp.where(zpos >= 1, pltpu.roll(prod[2 * ish:], 1, 1), 0.0)
        return (prod[ish:2 * ish] + low + high).astype(jnp.bfloat16)

    for s in range(1, nx):
        gsend[s] = shifted(xpeer(s))
        gi_copy(s).start()
    grecv[g] = shifted(g)

    for s in range(1, nx):
        gi_copy(s).wait_recv()
    full = grecv[...].reshape(nx * ish, cells).astype(jnp.float32)
    out_ref[...] = full.T.astype(jnp.bfloat16).reshape(sx, sy, sz, nx * ish)
    for k, chunk in enumerate(chunks):
        w = widths[k]
        total = red[k, z, :, pl.ds(0, w)]
        for s in range(1, nz):
            rs_copy(k, s, w).wait_recv()
            total = total + rs[k, s, :, pl.ds(0, w)]
        block = total * scale
        for j, ab in enumerate(chunk):
            for c in range(3):
                lane = j * rows + c * ish
                wg_ref[3 * ab + c] = block[:, lane:lane + ish]

    for s in range(1, nx):
        gat[s].wait_send()
        acts[s].wait_send()
        gi_copy(s).wait_send()

    @pl.when(h < ny - 1)
    def _():
        for s in range(nx):
            halo(s, True).wait_send()

    @pl.when(h > 0)
    def _():
        for s in range(nx):
            halo(s, False).wait_send()

    for k in range(len(chunks)):
        pair_copy(k, widths[k]).wait_send()
        for s in range(1, nz):
            rs_copy(k, s, widths[k]).wait_send()


def body(nx, ny, grad_out, relu_mask, activations, weight):
    sx, sy, sz, co = grad_out.shape
    ish = weight.shape[1]
    rows = 3 * ish
    cells = sx * sy * sz
    nz = ny // 2
    nch = -(-9 // PER)
    wide = -(-PER * rows // 128) * 128
    scale = 1.0 / math.sqrt(cells * nx * ny)
    dma = pltpu.SemaphoreType.DMA
    bf, f32 = jnp.bfloat16, jnp.float32
    any_spec = pl.BlockSpec(memory_space=pl.ANY)
    vmem_spec = pl.BlockSpec(memory_space=pltpu.VMEM)
    out, wg = pl.pallas_call(
        functools.partial(kernel, nx, ny, scale),
        out_shape=(jax.ShapeDtypeStruct((sx, sy, sz, nx * ish), bf),
                   jax.ShapeDtypeStruct((27, co // ny, ish), f32)),
        in_specs=[any_spec] * 4,
        out_specs=(vmem_spec, vmem_spec),
        scratch_shapes=[
            pltpu.VMEM((sx, sy, sz, co), bf),
            pltpu.VMEM((sx, sy, sz, co), jnp.int32),
            pltpu.VMEM((sx, sy, sz, nx * ish), bf),
            pltpu.VMEM((nx, ish, cells), bf),
            pltpu.VMEM((sx * nx + 2, sy + 2, sz, co), bf),
            pltpu.VMEM((nx, ish, cells), bf),
            pltpu.VMEM((nx, rows, cells), bf),
            pltpu.VMEM((27, ish, co), bf),
            pltpu.VMEM((nch, wide, co), f32),
            pltpu.VMEM((nch, nz, 2, co // ny, wide), f32),
            pltpu.VMEM((nch, nz, co // ny, wide), f32),
            pltpu.VMEM((nch, nz, co // ny, wide), f32),
            pltpu.VMEM((nch, nz, co // ny, wide), f32),
            pltpu.VMEM((nx, ish, cells), bf),
            pltpu.VMEM((nx, ish, cells), bf),
            dma((4,)), dma((nx,)), dma((nx,)), dma((nx,)), dma((nx,)),
            dma((2, nx)), dma((2, nx)), dma((nch,)), dma((nch,)),
            dma((nch, nz)), dma((nch, nz)), dma((nx,)), dma((nx,)),
        ],
        compiler_params=pltpu.CompilerParams(
            collective_id=0, has_side_effects=True, vmem_limit_bytes=60 * 1024 * 1024),
        name="conv_backward",
    )(grad_out, relu_mask, activations, weight)
    return out, jnp.transpose(wg, (0, 2, 1))


def solution(mesh):
    nx, ny = mesh.shape["gx"], mesh.shape["gy"]
    in_specs = (
        P("gx", "gy", None, None),
        P("gx", "gy", None, None),
        P("gx", "gy", None, None),
        P(None, "gx", None),
    )
    out_specs = (P("gx", "gy", None, None), P(None, "gx", "gy"))
    return jax.shard_map(
        functools.partial(body, nx, ny), mesh=mesh, in_specs=in_specs, out_specs=out_specs,
        check_vma=False)
```
